32 devices in a mesh: rep: 4 (over y, x), shard: 8 (over z, core).
Axes of the slice: x: 2, y: 2, z: 4, core: 2. Of those that a mesh axis runs over, the one named last changes fastest.
Arguments:
- tokens: bfloat16 [4096, 1024], P(('rep', 'shard')), may hold values from -6 to 6
- cotangent: float32 [4096, 1024], P(('rep', 'shard')), may hold values from -6 to 6
- lengths: int32 [32, 4], P(('rep', 'shard')), may hold values from 1 to 125, as said below
- in_weight: float32 [2, 1024, 2320], P(None, 'shard'), may hold values from -0.1875 to 0.1875
- out_weight: float32 [2, 1024, 1024], P(None, 'shard'), may hold values from -0.1875 to 0.1875
- small_params: float32 [2, 8496], replicated, may hold values from -6.91 to 2.78
- in_first: float32 [2, 1024, 2320], P(None, 'shard'), may hold values from -8 to 8
- in_second: float32 [2, 1024, 2320], P(None, 'shard'), may hold values from 1 to 100
- out_first: float32 [2, 1024, 1024], P(None, 'shard'), may hold values from -8 to 8
- out_second: float32 [2, 1024, 1024], P(None, 'shard'), may hold values from 1 to 100
- small_first: float32 [2, 8496], replicated, may hold values from -8 to 8
- small_second: float32 [2, 8496], replicated, may hold values from 1 to 100
Outputs:
- outputs: bfloat16 [4096, 1024], P(('rep', 'shard'))
- input_grad: float32 [4096, 1024], P(('rep', 'shard'))
- in_grad: float32 [2, 1024, 2320], P(None, 'shard')
- out_grad: float32 [2, 1024, 1024], P(None, 'shard')
- small_grad: float32 [2, 8496], replicated
- new_in: float32 [2, 1024, 2320], P(None, 'shard')
- new_out: float32 [2, 1024, 1024], P(None, 'shard')
- new_small: float32 [2, 8496], replicated
- new_in_first: float32 [2, 1024, 2320], P(None, 'shard')
- new_in_second: float32 [2, 1024, 2320], P(None, 'shard')
- new_out_first: float32 [2, 1024, 1024], P(None, 'shard')
- new_out_second: float32 [2, 1024, 1024], P(None, 'shard')
- new_small_first: float32 [2, 8496], replicated
- new_small_second: float32 [2, 8496], replicated
The draws below stay inside these ranges and needn't reach their ends.
Inputs may be any that keep to these rules, and one draw needn't show every extreme that they name: Each row's lengths sum to at most 128; row 0 sums to exactly 128.
All inputs are finite; a program needn't handle non-finite values.
Results may differ from the reference program's by a relative error of at most 0.013.
The reference program's roundings to bfloat16 on the way count: a program that leaves them out, or rounds other values in their place, can miss the bound.
Values may be sent and summed in bfloat16 or wider, within the bound.
A program may use at most 192 MiB of HBM per device.

```python
import math
import jax
import jax.numpy as jnp
from jax import lax

D = 1024
HEADS = 16
HEAD_DIM = 64
INNER = 1024
STATE = 128
KERNEL = 4
LAYERS = 2
TOK_DEV = 128
SEQ_DEV = 4
SEQ_ROWS = 32
TOKENS = 4096
CONV_CH = 1280
IN_WIDTH = 2320
SMALL = 8496


def draw_lengths(key, part):
    key_total, key_share = jax.random.split(key)
    rows_index = jnp.arange(SEQ_ROWS, dtype=jnp.int32)[:, None]
    column = jnp.arange(SEQ_DEV, dtype=jnp.int32)[None, :]
    spare = jax.random.randint(key_total, (SEQ_ROWS, 1), 0, TOK_DEV // 2 + 1)
    spare = jnp.where(rows_index == 0, 0, spare)
    totals = TOK_DEV - spare
    weights = jax.random.randint(key_share, (SEQ_ROWS, SEQ_DEV), 1, 64)
    weights = jnp.where((rows_index == 0) & (column < SEQ_DEV - 1), 0, weights)
    room = totals - SEQ_DEV
    shares = room * weights // jnp.sum(weights, axis=1, keepdims=True)
    leftover = room - jnp.sum(shares, axis=1, keepdims=True)
    shares = shares + jnp.where(column == SEQ_DEV - 1, leftover, 0)
    return (1 + shares).astype(jnp.int32)


def normal_like(key, count, scale):
    return jnp.clip(jax.random.normal(key, (count,), jnp.float32), -3.0, 3.0) * scale


def draw_layer(key):
    keys = jax.random.split(key, 7)
    pre_gain = jax.random.uniform(keys[0], (D,), jnp.float32, 0.75, 1.25)
    conv_weight = normal_like(keys[1], CONV_CH * KERNEL, 0.5)
    conv_bias = normal_like(keys[2], CONV_CH, 0.5)
    step_init = jnp.exp(jax.random.uniform(keys[3], (HEADS,), jnp.float32, math.log(0.001), math.log(0.1)))
    dt_bias = jnp.log(jnp.expm1(step_init))
    a_log = jnp.log(jax.random.uniform(keys[4], (HEADS,), jnp.float32, 1.0, 16.0))
    skip = jax.random.uniform(keys[5], (HEADS,), jnp.float32, 0.5, 1.5)
    norm_gain = jax.random.uniform(keys[6], (INNER,), jnp.float32, 0.75, 1.25)
    return jnp.concatenate([pre_gain, conv_weight, conv_bias, dt_bias, a_log, skip, norm_gain])


def draw_small_params(key, part):
    return jnp.stack([draw_layer(jax.random.fold_in(key, 11 + layer_idx)) for layer_idx in range(LAYERS)]).astype(jnp.float32)


def shard_levels(stream_key, dims, cuts, least, high):
    loudness, own = 1.0, jax.random.fold_in(stream_key, 6)
    for dim, blocks in cuts:
        steps = jnp.exp(jax.random.uniform(jax.random.fold_in(own, dim), (blocks,), jnp.float32, least / len(cuts), high / len(cuts)))
        loudness = loudness * jnp.repeat(steps, dims[dim] // blocks).reshape([-1 if axis == dim else 1 for axis in range(len(dims))])
    return loudness


def gaussian(key, dims, scale, bound, cuts=(), kind=jnp.bfloat16):
    values = jax.random.normal(key, dims, jnp.float32) * scale
    if len(cuts) > 0:
        values = shard_levels(key, dims, cuts, -0.22, 0.18) * values
    return jnp.clip(values, min=-bound, max=bound).astype(kind)


def setup_inputs(seed: int = 0) -> dict:
    splits = jax.random.split(jax.random.key(seed), 13)
    return {
        "tokens": gaussian(splits[0], (TOKENS, D), 1.0, 6.0, ((0, 32),)),
        "cotangent": gaussian(splits[1], (TOKENS, D), 1.0, 6.0, ((0, 32),), jnp.float32),
        "lengths": draw_lengths(jax.random.fold_in(splits[12], 71), 0),
        "in_weight": gaussian(splits[3], (LAYERS, D, IN_WIDTH), D ** -0.5, 0.1875, ((1, 8),), jnp.float32),
        "out_weight": gaussian(splits[4], (LAYERS, INNER, D), INNER ** -0.5, 0.1875, ((1, 8),), jnp.float32),
        "small_params": draw_small_params(jax.random.fold_in(splits[12], 71), 0),
        "in_first": gaussian(splits[6], (LAYERS, D, IN_WIDTH), 2.0, 8.0, ((1, 8),), jnp.float32),
        "in_second": jnp.clip(jnp.exp(math.log(100.0) - 4.6051702 * jax.random.uniform(splits[7], (LAYERS, D, IN_WIDTH), jnp.float32) ** shard_levels(splits[7], (LAYERS, D, IN_WIDTH), ((1, 8),), -0.2, 0.2)), 1.0, 100.0),
        "out_first": gaussian(splits[8], (LAYERS, INNER, D), 2.0, 8.0, ((1, 8),), jnp.float32),
        "out_second": jnp.clip(jnp.exp(math.log(100.0) - 4.6051702 * jax.random.uniform(splits[9], (LAYERS, INNER, D), jnp.float32) ** shard_levels(splits[9], (LAYERS, INNER, D), ((1, 8),), -0.2, 0.2)), 1.0, 100.0),
        "small_first": gaussian(splits[10], (LAYERS, SMALL), 2.0, 8.0, (), jnp.float32),
        "small_second": jnp.clip(jnp.exp(jax.random.uniform(splits[11], (LAYERS, SMALL), jnp.float32, math.log(1.0), math.log(100.0))), 1.0, 100.0),
    }


norm_eps = 1e-05
beta_one = 0.9
beta_two = 0.95
adam_eps = 1e-08
learning_rate = 0.1
weight_decay = 0.1
step_count = 3

def small_shapes():
    return [(D,), (CONV_CH, KERNEL), (CONV_CH,), (HEADS,), (HEADS,), (HEADS,), (INNER,)]

def split_small(flat_row):
    pieces = []
    offset = 0
    for piece_dims in small_shapes():
        length = math.prod(piece_dims)
        pieces.append(flat_row[offset:offset + length].reshape(piece_dims))
        offset = offset + length
    return pieces

def segment_ids(seq_lens, row_count):
    seq_ends = jnp.cumsum(seq_lens).astype(jnp.int32)
    places = jnp.arange(row_count, dtype=jnp.int32)
    return lax.optimization_barrier(jnp.sum((places[:, None] >= seq_ends[None, :]).astype(jnp.int32), axis=1)).astype(jnp.int32)

def prenorm(stream, gain):
    return stream * lax.rsqrt(lax.optimization_barrier(jnp.mean(stream * stream, axis=-1, keepdims=True)) + norm_eps) * gain

def ssd_mixer(projected, conv_weight, conv_bias, dt_bias, a_log, skip, norm_gain, segment):
    row_count = projected.shape[0]
    gate_in = projected[:, :INNER]
    conv_in = projected[:, INNER:INNER + CONV_CH]
    dt_raw = projected[:, INNER + CONV_CH:]
    conv_out = conv_bias[None, :] + conv_weight[None, :, KERNEL - 1] * conv_in
    for lag_steps in range(1, KERNEL):
        shifted = jnp.concatenate([jnp.zeros((lag_steps, CONV_CH), jnp.float32), conv_in[:-lag_steps]], axis=0)
        earlier = jnp.concatenate([jnp.full((lag_steps,), -1, jnp.int32), segment[:-lag_steps]], axis=0)
        conv_out = conv_out + conv_weight[None, :, KERNEL - 1 - lag_steps] * jnp.where((earlier == segment)[:, None], shifted, 0.0)
    activated = jax.nn.silu(conv_out)
    values = activated[:, :INNER].reshape(row_count, HEADS, HEAD_DIM)
    b_state = activated[:, INNER:INNER + STATE]
    c_state = activated[:, INNER + STATE:]
    step_size = jax.nn.softplus(dt_raw + dt_bias[None, :])
    log_decay = -jnp.exp(a_log)[None, :] * step_size
    cumulative = jnp.cumsum(log_decay, axis=0)
    scores = jnp.dot(c_state, b_state.T, precision=lax.Precision.HIGHEST)
    places = jnp.arange(row_count, dtype=jnp.int32)
    allowed = ((places[:, None] >= places[None, :]) & (segment[:, None] == segment[None, :]))[None]
    spread = cumulative.T[:, :, None] - cumulative.T[:, None, :]
    decays = jnp.where(allowed, jnp.exp(jnp.where(allowed, spread, 0.0)), 0.0)
    kernel_mat = decays * scores[None] * step_size.T[:, None, :]
    output = jnp.einsum('hts,shp->thp', kernel_mat, values, precision=lax.Precision.HIGHEST)
    output = output + skip[None, :, None] * values
    gated_out = output.reshape(row_count, INNER) * jax.nn.silu(gate_in)
    return gated_out * lax.rsqrt(lax.optimization_barrier(jnp.mean(gated_out * gated_out, axis=-1, keepdims=True)) + norm_eps) * norm_gain

def forward_layer(stream, in_wide, out_wide, small_pieces, segment):
    normed = prenorm(stream, small_pieces[0]).astype(jnp.bfloat16)
    projected = jnp.dot(normed, in_wide, preferred_element_type=jnp.float32)
    mixed_out = ssd_mixer(projected, *small_pieces[1:], segment).astype(jnp.bfloat16)
    result = stream + jnp.dot(mixed_out, out_wide, preferred_element_type=jnp.float32)
    return (result, (normed, projected, mixed_out))

def backward_layer(stream, kept_acts, in_wide, out_wide, small_pieces, segment, upstream):
    normed, projected, mixed_out = kept_acts
    grad_bf = upstream.astype(jnp.bfloat16)
    grad_mixed = lax.dot_general(grad_bf, out_wide, (((1,), (1,)), ((), ())), preferred_element_type=jnp.float32)
    grad_out_weight = lax.dot_general(mixed_out, grad_bf, (((0,), (0,)), ((), ())), preferred_element_type=jnp.float32)

    def local_mixer(proj_in, *small_in):
        return ssd_mixer(proj_in, *small_in, segment)
    unused, pull_back = jax.vjp(local_mixer, projected, *small_pieces[1:])
    pulled = pull_back(grad_mixed)
    grad_proj = pulled[0].astype(jnp.bfloat16)
    grad_normed = lax.dot_general(grad_proj, in_wide, (((1,), (1,)), ((), ())), preferred_element_type=jnp.float32)
    grad_in_weight = lax.dot_general(normed, grad_proj, (((0,), (0,)), ((), ())), preferred_element_type=jnp.float32)
    unused_norm, pull_norm = jax.vjp(prenorm, stream, small_pieces[0])
    grad_stream, grad_gain = pull_norm(grad_normed)
    small_flat = jnp.concatenate([grad_gain] + [term.reshape(-1) for term in pulled[1:]])
    return (upstream + grad_stream, grad_in_weight, grad_out_weight, small_flat)

def block_pass(tokens_block, cot_block, seq_lens, in_wide, out_wide, small_rows):
    segment = segment_ids(seq_lens, tokens_block.shape[0])
    stream = tokens_block.astype(jnp.float32)
    inputs_kept = []
    acts_kept = []
    for layer_idx in range(LAYERS):
        inputs_kept.append(stream)
        stream, kept_acts = forward_layer(stream, in_wide[layer_idx], out_wide[layer_idx], split_small(small_rows[layer_idx]), segment)
        acts_kept.append(kept_acts)
    result = stream.astype(jnp.bfloat16)
    upstream = cot_block * (segment < SEQ_DEV).astype(jnp.float32)[:, None]
    in_rows = [None] * LAYERS
    out_rows = [None] * LAYERS
    small_rows_grad = [None] * LAYERS
    for layer_idx in reversed(range(LAYERS)):
        upstream, in_rows[layer_idx], out_rows[layer_idx], small_rows_grad[layer_idx] = backward_layer(inputs_kept[layer_idx], acts_kept[layer_idx], in_wide[layer_idx], out_wide[layer_idx], split_small(small_rows[layer_idx]), segment, upstream)
    return (result, upstream, (jnp.stack(in_rows), jnp.stack(out_rows), jnp.stack(small_rows_grad)))

def adamw_update(params, grad_rows, first_state, second_state):
    new_first = beta_one * first_state + (1.0 - beta_one) * grad_rows
    new_second = beta_two * second_state + (1.0 - beta_two) * grad_rows * grad_rows
    first_hat = new_first / (1.0 - beta_one ** step_count)
    second_hat = new_second / (1.0 - beta_two ** step_count)
    new_params = params - learning_rate * (first_hat / (jnp.sqrt(second_hat) + adam_eps) + weight_decay * params)
    return (new_params, new_first, new_second)

def reference(tokens, cotangent, lengths, in_weight, out_weight, small_params, in_first, in_second, out_first, out_second, small_first, small_second):
    in_wide = in_weight.astype(jnp.bfloat16)
    out_wide = out_weight.astype(jnp.bfloat16)
    small_rows = lax.optimization_barrier(small_params.astype(jnp.bfloat16)).astype(jnp.float32)

    def scan_step(totals, inputs):
        tokens_block, cot_block, seq_lens = inputs
        result, input_grad, grads = block_pass(tokens_block, cot_block, seq_lens, in_wide, out_wide, small_rows)
        return ((totals[0] + grads[0], totals[1] + grads[1], totals[2] + grads[2]), (result, input_grad))
    start = (jnp.zeros((LAYERS, D, IN_WIDTH), jnp.float32), jnp.zeros((LAYERS, INNER, D), jnp.float32), jnp.zeros((LAYERS, SMALL), jnp.float32))
    totals, (results, input_grads) = lax.scan(scan_step, start, (tokens.reshape(SEQ_ROWS, TOK_DEV, D), cotangent.reshape(SEQ_ROWS, TOK_DEV, D), lengths))
    in_grad, out_grad, small_grad = totals
    new_in, new_in_first, new_in_second = adamw_update(in_weight, in_grad, in_first, in_second)
    new_out, new_out_first, new_out_second = adamw_update(out_weight, out_grad, out_first, out_second)
    new_small, new_small_first, new_small_second = adamw_update(small_params, small_grad, small_first, small_second)
    return (results.reshape(TOKENS, D), input_grads.reshape(TOKENS, D), in_grad, out_grad, small_grad, new_in, new_out, new_small, new_in_first, new_in_second, new_out_first, new_out_second, new_small_first, new_small_second)
```

```python
import math

import jax
import jax.numpy as jnp
from jax import lax
from jax.sharding import PartitionSpec as P

D = 1024
HEADS = 16
HEAD_DIM = 64
INNER = 1024
STATE = 128
KERNEL = 4
LAYERS = 2
SEQ_DEV = 4
CONV_CH = 1280


norm_eps = 1e-05
beta_one = 0.9
beta_two = 0.95
adam_eps = 1e-08
learning_rate = 0.1
weight_decay = 0.1
step_count = 3


def small_shapes():
    return [(D,), (CONV_CH, KERNEL), (CONV_CH,), (HEADS,), (HEADS,), (HEADS,), (INNER,)]


def split_small(flat_row):
    pieces = []
    offset = 0
    for piece_dims in small_shapes():
        length = math.prod(piece_dims)
        pieces.append(flat_row[offset : offset + length].reshape(piece_dims))
        offset = offset + length
    return pieces


def segment_ids(seq_lens, row_count):
    seq_ends = jnp.cumsum(seq_lens)
    places = jnp.arange(row_count, dtype=jnp.int32)
    return jnp.sum((places[:, None] >= seq_ends[None, :]).astype(jnp.int32), axis=1)


def prenorm(stream, gain):
    return stream * lax.rsqrt(jnp.mean(stream * stream, axis=-1, keepdims=True) + norm_eps) * gain


def ssd_mixer(projected, conv_weight, conv_bias, dt_bias, a_log, skip, norm_gain, segment):
    row_count = projected.shape[0]
    gate_in = projected[:, :INNER]
    conv_in = projected[:, INNER : INNER + CONV_CH]
    dt_raw = projected[:, INNER + CONV_CH :]
    conv_out = conv_bias[None, :] + conv_weight[None, :, KERNEL - 1] * conv_in
    for lag_steps in range(1, KERNEL):
        shifted = jnp.concatenate(
            [jnp.zeros((lag_steps, CONV_CH), jnp.float32), conv_in[:-lag_steps]], axis=0
        )
        earlier = jnp.concatenate(
            [jnp.full((lag_steps,), -1, jnp.int32), segment[:-lag_steps]], axis=0
        )
        conv_out = conv_out + conv_weight[None, :, KERNEL - 1 - lag_steps] * jnp.where(
            (earlier == segment)[:, None], shifted, 0.0
        )
    activated = jax.nn.silu(conv_out)
    values = activated[:, :INNER].reshape(row_count, HEADS, HEAD_DIM)
    b_state = activated[:, INNER : INNER + STATE]
    c_state = activated[:, INNER + STATE :]
    step_size = jax.nn.softplus(dt_raw + dt_bias[None, :])
    log_decay = -jnp.exp(a_log)[None, :] * step_size
    cumulative = jnp.cumsum(log_decay, axis=0)
    scores = jnp.dot(c_state, b_state.T, precision=lax.Precision.HIGHEST)
    places = jnp.arange(row_count, dtype=jnp.int32)
    allowed = ((places[:, None] >= places[None, :]) & (segment[:, None] == segment[None, :]))[None]
    spread = cumulative.T[:, :, None] - cumulative.T[:, None, :]
    decays = jnp.where(allowed, jnp.exp(jnp.where(allowed, spread, 0.0)), 0.0)
    kernel_mat = decays * scores[None] * step_size.T[:, None, :]
    output = jnp.einsum("hts,shp->thp", kernel_mat, values, precision=lax.Precision.HIGHEST)
    output = output + skip[None, :, None] * values
    gated_out = output.reshape(row_count, INNER) * jax.nn.silu(gate_in)
    return (
        gated_out
        * lax.rsqrt(jnp.mean(gated_out * gated_out, axis=-1, keepdims=True) + norm_eps)
        * norm_gain
    )


def forward_layer(stream, in_wide, out_wide, small_pieces, segment):
    normed = prenorm(stream, small_pieces[0]).astype(jnp.bfloat16)
    projected = jnp.dot(normed, in_wide, preferred_element_type=jnp.float32)
    mixed_out = ssd_mixer(projected, *small_pieces[1:], segment).astype(jnp.bfloat16)
    result = stream + jnp.dot(mixed_out, out_wide, preferred_element_type=jnp.float32)
    return (result, (normed, projected, mixed_out))


def adamw_update(params, grad_rows, first_state, second_state):
    new_first = beta_one * first_state + (1.0 - beta_one) * grad_rows
    new_second = beta_two * second_state + (1.0 - beta_two) * grad_rows * grad_rows
    first_hat = new_first / (1.0 - beta_one**step_count)
    second_hat = new_second / (1.0 - beta_two**step_count)
    new_params = params - learning_rate * (
        first_hat / (jnp.sqrt(second_hat) + adam_eps) + weight_decay * params
    )
    return (new_params, new_first, new_second)


def swap(value, axis, bit, size):
    return lax.ppermute(value, axis, [(spot, spot ^ bit) for spot in range(size)])


def turn(value, step, size):
    return lax.ppermute(value, "shard", [(spot, (spot + step) % size) for spot in range(size)])


def pick(value, index, axis):
    return lax.dynamic_index_in_dim(value, index, axis, keepdims=False)


def in_order(mine, other, index, axis):
    first = jnp.where(index == 0, mine, other)
    second = jnp.where(index == 0, other, mine)
    return jnp.stack([first, second], axis)


def places():
    rep, shard = lax.axis_index("rep"), lax.axis_index("shard")
    return rep % 2, rep // 2, shard // 2, shard % 2


def staged():
    return lax.axis_size("rep") == 4 and lax.axis_size("shard") % 2 == 0


def gather_rows(rows):
    if not staged():
        return lax.all_gather(rows, "shard", axis=0, tiled=True)
    at_x, at_y, at_z, at_core = places()
    shards, reps = lax.axis_size("shard"), lax.axis_size("rep")
    chips = shards // 2
    count, width = rows.shape
    pieces = rows.reshape(2, 2, 2, count // 8, width)
    own = jnp.stack([pick(pick(pieces[0], at_x, 0), at_y, 0), pick(pick(pieces[1], at_y, 0), at_x, 0)])
    by_turn = [own] + [turn(own, 2 * step, shards) for step in range(1, chips)]
    stacked = jnp.stack(by_turn[::-1] + by_turn[::-1][:-1])
    along = lax.dynamic_slice_in_dim(stacked, chips - 1 - at_z, chips, 0)
    near_x, near_y = along[:, 0], along[:, 1]
    far_x = swap(near_x, "rep", 2, reps)
    far_y = swap(near_y, "rep", 1, reps)
    pair_x = in_order(near_x, far_x, at_y, 1)
    pair_y = in_order(near_y, far_y, at_x, 1)
    other_x = swap(pair_x, "rep", 1, reps)
    other_y = swap(pair_y, "rep", 2, reps)
    half = jnp.stack([in_order(pair_x, other_x, at_x, 1), in_order(pair_y, other_y, at_y, 1)], 1)
    half = half.reshape(chips, count, width)
    other = swap(half, "shard", 1, shards)
    return in_order(half, other, at_core, 1).reshape(shards * count, width)


def total_rows(left, right):
    if not staged():
        whole = lax.dot_general(
            left, right, (((0,), (0,)), ((), ())), preferred_element_type=jnp.float32
        )
        owned = lax.psum_scatter(whole, "shard", scatter_dimension=0, tiled=True)
        return lax.psum(owned, "rep")
    at_x, at_y, at_z, at_core = places()
    shards, reps = lax.axis_size("shard"), lax.axis_size("rep")
    chips = shards // 2
    count, width = left.shape[1] // shards, right.shape[1]
    split = left.reshape(left.shape[0], chips, 2, count)

    def product(core):
        part = pick(split, core, 2).reshape(left.shape[0], chips * count)
        return lax.dot_general(
            part, right, (((0,), (0,)), ((), ())), preferred_element_type=jnp.float32
        )

    received = swap(product(1 - at_core).astype(jnp.bfloat16), "shard", 1, shards)
    summed = product(at_core) + received.astype(jnp.float32)
    summed = summed.reshape(chips, 2, 2, 2, count // 8, width)
    from_x = swap(pick(summed[:, 0], 1 - at_x, 1).astype(jnp.bfloat16), "rep", 1, reps)
    from_y = swap(pick(summed[:, 1], 1 - at_y, 1).astype(jnp.bfloat16), "rep", 2, reps)
    one = pick(summed[:, 0], at_x, 1) + from_x.astype(jnp.float32)
    two = pick(summed[:, 1], at_y, 1) + from_y.astype(jnp.float32)
    from_y = swap(pick(one, 1 - at_y, 1).astype(jnp.bfloat16), "rep", 2, reps)
    from_x = swap(pick(two, 1 - at_x, 1).astype(jnp.bfloat16), "rep", 1, reps)
    one = pick(one, at_y, 1) + from_y.astype(jnp.float32)
    two = pick(two, at_x, 1) + from_x.astype(jnp.float32)
    square = jnp.stack([one, two], 1)
    owned = pick(square, at_z, 0)
    for step in range(1, chips):
        going = pick(square, (at_z + step) % chips, 0).astype(jnp.bfloat16)
        owned = owned + turn(going, 2 * step, shards).astype(jnp.float32)
    owned = owned.astype(jnp.bfloat16)
    one, two = owned[0], owned[1]
    far_x = swap(one, "rep", 2, reps)
    far_y = swap(two, "rep", 1, reps)
    pair_x = in_order(one, far_x, at_y, 0)
    pair_y = in_order(two, far_y, at_x, 0)
    other_x = swap(pair_x, "rep", 1, reps)
    other_y = swap(pair_y, "rep", 2, reps)
    whole = jnp.stack([in_order(pair_x, other_x, at_x, 0), in_order(pair_y, other_y, at_y, 0)])
    return whole.reshape(count, width)


def total_small(flat):
    shards, reps = lax.axis_size("shard"), lax.axis_size("rep")
    if not staged() or shards & (shards - 1):
        return lax.psum(flat, ("rep", "shard"))
    for axis, size in (("shard", shards), ("rep", reps)):
        bit = 1
        while bit < size:
            flat = flat + swap(flat, axis, bit, size)
            bit = 2 * bit
    return flat


def on_device(
    tokens,
    cotangent,
    lengths,
    in_weight,
    out_weight,
    small_params,
    in_first,
    in_second,
    out_first,
    out_second,
    small_first,
    small_second,
):
    segment = segment_ids(lengths[0], tokens.shape[0])
    small_rows = lax.optimization_barrier(small_params.astype(jnp.bfloat16)).astype(jnp.float32)
    stream = tokens.astype(jnp.float32)
    kept_weights = []
    inputs_kept = []
    acts_kept = []
    for layer_idx in range(LAYERS):
        gathered = (
            gather_rows(in_weight[layer_idx].astype(jnp.bfloat16)),
            gather_rows(out_weight[layer_idx].astype(jnp.bfloat16)),
        )
        kept_weights.append(gathered)
        inputs_kept.append(stream)
        stream, kept_acts = forward_layer(
            stream, gathered[0], gathered[1], split_small(small_rows[layer_idx]), segment
        )
        acts_kept.append(kept_acts)
    result = stream.astype(jnp.bfloat16)
    upstream = cotangent * (segment < SEQ_DEV).astype(jnp.float32)[:, None]
    in_rows = [None] * LAYERS
    out_rows = [None] * LAYERS
    small_sums = [None] * LAYERS
    for layer_idx in reversed(range(LAYERS)):
        in_wide, out_wide = kept_weights[layer_idx]
        normed, projected, mixed_out = acts_kept[layer_idx]
        small_pieces = split_small(small_rows[layer_idx])
        grad_bf = upstream.astype(jnp.bfloat16)
        grad_mixed = lax.dot_general(
            grad_bf, out_wide, (((1,), (1,)), ((), ())), preferred_element_type=jnp.float32
        )

        def local_mixer(proj_in, *small_in):
            return ssd_mixer(proj_in, *small_in, segment)

        unused, pull_back = jax.vjp(local_mixer, projected, *small_pieces[1:])
        pulled = pull_back(grad_mixed)
        grad_proj = pulled[0].astype(jnp.bfloat16)
        grad_normed = lax.dot_general(
            grad_proj, in_wide, (((1,), (1,)), ((), ())), preferred_element_type=jnp.float32
        )
        unused_norm, pull_norm = jax.vjp(prenorm, inputs_kept[layer_idx], small_pieces[0])
        grad_stream, grad_gain = pull_norm(grad_normed)
        small_flat = jnp.concatenate([grad_gain] + [term.reshape(-1) for term in pulled[1:]])

        in_rows[layer_idx] = total_rows(normed, grad_proj)
        out_rows[layer_idx] = total_rows(mixed_out, grad_bf)
        small_sums[layer_idx] = total_small(small_flat)
        upstream = upstream + grad_stream
    in_grad = jnp.stack(in_rows).astype(jnp.float32)
    out_grad = jnp.stack(out_rows).astype(jnp.float32)
    small_grad = jnp.stack(small_sums)
    new_in, new_in_first, new_in_second = adamw_update(in_weight, in_grad, in_first, in_second)
    new_out, new_out_first, new_out_second = adamw_update(
        out_weight, out_grad, out_first, out_second
    )
    new_small, new_small_first, new_small_second = adamw_update(
        small_params, small_grad, small_first, small_second
    )
    return (
        result,
        upstream,
        in_grad,
        out_grad,
        small_grad,
        new_in,
        new_out,
        new_small,
        new_in_first,
        new_in_second,
        new_out_first,
        new_out_second,
        new_small_first,
        new_small_second,
    )


def solution(mesh):
    return jax.shard_map(
        on_device,
        mesh=mesh,
        in_specs=(
            P(("rep", "shard"), None),
            P(("rep", "shard"), None),
            P(("rep", "shard"), None),
            P(None, "shard", None),
            P(None, "shard", None),
            P(),
            P(None, "shard", None),
            P(None, "shard", None),
            P(None, "shard", None),
            P(None, "shard", None),
            P(),
            P(),
        ),
        out_specs=(
            P(("rep", "shard"), None),
            P(("rep", "shard"), None),
            P(None, "shard", None),
            P(None, "shard", None),
            P(),
            P(None, "shard", None),
            P(None, "shard", None),
            P(),
            P(None, "shard", None),
            P(None, "shard", None),
            P(None, "shard", None),
            P(None, "shard", None),
            P(),
            P(),
        ),
        check_vma=False,
    )
```

```python
import math

import jax
import jax.numpy as jnp
from jax import lax
from jax.experimental import pallas as pl
from jax.experimental.pallas import tpu as pltpu
from jax.sharding import PartitionSpec as P

D = 1024
HEADS = 16
HEAD_DIM = 64
INNER = 1024
STATE = 128
KERNEL = 4
LAYERS = 2
SEQ_DEV = 4
CONV_CH = 1280


norm_eps = 1e-05
beta_one = 0.9
beta_two = 0.95
adam_eps = 1e-08
learning_rate = 0.1
weight_decay = 0.1
step_count = 3


def small_shapes():
    return [(D,), (CONV_CH, KERNEL), (CONV_CH,), (HEADS,), (HEADS,), (HEADS,), (INNER,)]


def split_small(flat_row):
    pieces = []
    offset = 0
    for piece_dims in small_shapes():
        length = math.prod(piece_dims)
        pieces.append(flat_row[offset : offset + length].reshape(piece_dims))
        offset = offset + length
    return pieces


def segment_ids(seq_lens, row_count):
    seq_ends = jnp.cumsum(seq_lens)
    places = jnp.arange(row_count, dtype=jnp.int32)
    return jnp.sum((places[:, None] >= seq_ends[None, :]).astype(jnp.int32), axis=1)


def prenorm(stream, gain):
    return stream * lax.rsqrt(jnp.mean(stream * stream, axis=-1, keepdims=True) + norm_eps) * gain


def ssd_mixer(projected, conv_weight, conv_bias, dt_bias, a_log, skip, norm_gain, segment):
    row_count = projected.shape[0]
    gate_in = projected[:, :INNER]
    conv_in = projected[:, INNER : INNER + CONV_CH]
    dt_raw = projected[:, INNER + CONV_CH :]
    conv_out = conv_bias[None, :] + conv_weight[None, :, KERNEL - 1] * conv_in
    for lag_steps in range(1, KERNEL):
        shifted = jnp.concatenate(
            [jnp.zeros((lag_steps, CONV_CH), jnp.float32), conv_in[:-lag_steps]], axis=0
        )
        earlier = jnp.concatenate(
            [jnp.full((lag_steps,), -1, jnp.int32), segment[:-lag_steps]], axis=0
        )
        conv_out = conv_out + conv_weight[None, :, KERNEL - 1 - lag_steps] * jnp.where(
            (earlier == segment)[:, None], shifted, 0.0
        )
    activated = jax.nn.silu(conv_out)
    values = activated[:, :INNER].reshape(row_count, HEADS, HEAD_DIM)
    b_state = activated[:, INNER : INNER + STATE]
    c_state = activated[:, INNER + STATE :]
    step_size = jax.nn.softplus(dt_raw + dt_bias[None, :])
    log_decay = -jnp.exp(a_log)[None, :] * step_size
    cumulative = jnp.cumsum(log_decay, axis=0)
    scores = jnp.dot(c_state, b_state.T, precision=lax.Precision.HIGHEST)
    places = jnp.arange(row_count, dtype=jnp.int32)
    allowed = ((places[:, None] >= places[None, :]) & (segment[:, None] == segment[None, :]))[None]
    spread = cumulative.T[:, :, None] - cumulative.T[:, None, :]
    decays = jnp.where(allowed, jnp.exp(jnp.where(allowed, spread, 0.0)), 0.0)
    kernel_mat = decays * scores[None] * step_size.T[:, None, :]
    output = jnp.einsum("hts,shp->thp", kernel_mat, values, precision=lax.Precision.HIGHEST)
    output = output + skip[None, :, None] * values
    gated_out = output.reshape(row_count, INNER) * jax.nn.silu(gate_in)
    return (
        gated_out
        * lax.rsqrt(jnp.mean(gated_out * gated_out, axis=-1, keepdims=True) + norm_eps)
        * norm_gain
    )


def forward_layer(stream, in_wide, out_wide, small_pieces, segment):
    normed = prenorm(stream, small_pieces[0]).astype(jnp.bfloat16)
    projected = jnp.dot(normed, in_wide, preferred_element_type=jnp.float32)
    mixed_out = ssd_mixer(projected, *small_pieces[1:], segment).astype(jnp.bfloat16)
    result = stream + jnp.dot(mixed_out, out_wide, preferred_element_type=jnp.float32)
    return (result, (normed, projected, mixed_out))


def adamw_update(params, grad_rows, first_state, second_state):
    new_first = beta_one * first_state + (1.0 - beta_one) * grad_rows
    new_second = beta_two * second_state + (1.0 - beta_two) * grad_rows * grad_rows
    first_hat = new_first / (1.0 - beta_one**step_count)
    second_hat = new_second / (1.0 - beta_two**step_count)
    new_params = params - learning_rate * (
        first_hat / (jnp.sqrt(second_hat) + adam_eps) + weight_decay * params
    )
    return (new_params, new_first, new_second)


def swap(value, axis, bit, size):
    return lax.ppermute(value, axis, [(spot, spot ^ bit) for spot in range(size)])


def turn(value, step, size):
    return lax.ppermute(value, "shard", [(spot, (spot + step) % size) for spot in range(size)])


def pick(value, index, axis):
    return lax.dynamic_index_in_dim(value, index, axis, keepdims=False)


def in_order(mine, other, index, axis):
    first = jnp.where(index == 0, mine, other)
    second = jnp.where(index == 0, other, mine)
    return jnp.stack([first, second], axis)


def places():
    rep, shard = lax.axis_index("rep"), lax.axis_index("shard")
    return rep % 2, rep // 2, shard // 2, shard % 2


def staged():
    return lax.axis_size("rep") == 4 and lax.axis_size("shard") % 2 == 0


def mesh_place(at_x, at_y, at_z, at_core):
    return (at_y * 2 + at_x, at_z * 2 + at_core)


def push(source, target, send, recv, slot, place):
    copy = pltpu.make_async_remote_copy(
        src_ref=source,
        dst_ref=target,
        send_sem=send.at[slot],
        recv_sem=recv.at[slot],
        device_id=place,
        device_id_type=pl.DeviceIdType.MESH,
    )
    copy.start()
    return copy


def greet(partners):
    barrier = pltpu.get_barrier_semaphore()
    for place in partners:
        pl.semaphore_signal(
            barrier, inc=1, device_id=place, device_id_type=pl.DeviceIdType.MESH
        )
    pl.semaphore_wait(barrier, len(partners))


def neighbours(chips):
    at_x, at_y, at_z, at_core = places()
    next_x = mesh_place(1 - at_x, at_y, at_z, at_core)
    next_y = mesh_place(at_x, 1 - at_y, at_z, at_core)
    twin = mesh_place(at_x, at_y, at_z, 1 - at_core)
    along = [
        mesh_place(at_x, at_y, lax.rem(at_z + step, chips), at_core) for step in range(1, chips)
    ]
    return next_x, next_y, twin, along


def gather_kernel(chips, count, *refs):
    own, whole = refs[:count], refs[count : 2 * count]
    send, recv, local = refs[2 * count :]
    at_x, at_y, at_z, at_core = places()
    next_x, next_y, twin, along = neighbours(chips)
    greet([next_x, next_y, twin] + along)
    first, second = (at_x, at_y), (at_y, at_x)
    inner, outer = (next_y, next_x), (next_x, next_y)
    started = []
    slots = iter(range(send.shape[0]))

    def go(source, target, place):
        copy = push(source, target, send, recv, next(slots), place)
        started.append(copy)
        return copy

    kept, level_one, level_four = [], {}, []
    for k in range(count):
        for step in range(1, chips):
            level_one[k, step] = [
                go(
                    own[k].at[h, first[h], second[h]],
                    whole[k].at[at_z, at_core, h, first[h], second[h]],
                    along[step - 1],
                )
                for h in range(2)
            ]
    for k in range(count):
        keep = pltpu.make_async_copy(own[k], whole[k].at[at_z, at_core], local.at[k])
        keep.start()
        kept.append(keep)
        level_four.append(go(own[k], whole[k].at[at_z, at_core], twin))
    units = [(k, step) for k in range(count) for step in range(1, chips)]
    level_two, level_three = {}, {}
    for turn_index in range(len(units) + 2):
        if turn_index < len(units):
            k, step = unit = units[turn_index]
            origin = lax.rem(at_z + chips - step, chips)
            level_two[unit] = []
            for h in range(2):
                level_one[unit][h].wait_recv()
                piece = whole[k].at[origin, at_core, h, first[h], second[h]]
                level_two[unit].append(go(piece, piece, inner[h]))
        if 0 <= turn_index - 1 < len(units):
            k, step = unit = units[turn_index - 1]
            origin = lax.rem(at_z + chips - step, chips)
            level_three[unit] = []
            for h in range(2):
                level_two[unit][h].wait_recv()
                piece = whole[k].at[origin, at_core, h, first[h]]
                level_three[unit].append(go(piece, piece, outer[h]))
        if 0 <= turn_index - 2:
            k, step = unit = units[turn_index - 2]
            origin = lax.rem(at_z + chips - step, chips)
            for h in range(2):
                level_three[unit][h].wait_recv()
            piece = whole[k].at[origin, at_core]
            level_four.append(go(piece, piece, twin))
    for copy in level_four:
        copy.wait_recv()
    for copy in started:
        copy.wait_send()
    for keep in kept:
        keep.wait()


def gather_all(shards_rows):
    if not staged():
        return [lax.all_gather(rows, "shard", axis=0, tiled=True) for rows in shards_rows]
    shards = lax.axis_size("shard")
    chips = shards // 2
    count = len(shards_rows)
    own = [rows.reshape(2, 2, 2, rows.shape[0] // 8, rows.shape[1]) for rows in shards_rows]
    copies = count * (7 * (chips - 1) + 1)
    whole = pl.pallas_call(
        lambda *refs: gather_kernel(chips, count, *refs),
        out_shape=[jax.ShapeDtypeStruct((chips, 2) + rows.shape, rows.dtype) for rows in own],
        in_specs=[pl.BlockSpec(memory_space=pltpu.VMEM)] * count,
        out_specs=[pl.BlockSpec(memory_space=pl.ANY)] * count,
        scratch_shapes=[
            pltpu.SemaphoreType.DMA((copies,)),
            pltpu.SemaphoreType.DMA((copies,)),
            pltpu.SemaphoreType.DMA((count,)),
        ],
        compiler_params=pltpu.CompilerParams(collective_id=0, has_side_effects=True),
        name="gather_all",
    )(*own)
    return [full.reshape(-1, rows.shape[1]) for full, rows in zip(whole, shards_rows)]


def total_rows(left, right):
    if not staged():
        whole = lax.dot_general(
            left, right, (((0,), (0,)), ((), ())), preferred_element_type=jnp.float32
        )
        owned = lax.psum_scatter(whole, "shard", scatter_dimension=0, tiled=True)
        return lax.psum(owned, "rep")
    at_x, at_y, at_z, at_core = places()
    shards, reps = lax.axis_size("shard"), lax.axis_size("rep")
    chips = shards // 2
    count, width = left.shape[1] // shards, right.shape[1]
    split = left.reshape(left.shape[0], chips, 2, count)

    def product(core):
        part = pick(split, core, 2).reshape(left.shape[0], chips * count)
        return lax.dot_general(
            part, right, (((0,), (0,)), ((), ())), preferred_element_type=jnp.float32
        )

    received = swap(product(1 - at_core).astype(jnp.bfloat16), "shard", 1, shards)
    summed = product(at_core) + received.astype(jnp.float32)
    summed = summed.reshape(chips, 2, 2, 2, count // 8, width)
    from_x = swap(pick(summed[:, 0], 1 - at_x, 1).astype(jnp.bfloat16), "rep", 1, reps)
    from_y = swap(pick(summed[:, 1], 1 - at_y, 1).astype(jnp.bfloat16), "rep", 2, reps)
    one = pick(summed[:, 0], at_x, 1) + from_x.astype(jnp.float32)
    two = pick(summed[:, 1], at_y, 1) + from_y.astype(jnp.float32)
    from_y = swap(pick(one, 1 - at_y, 1).astype(jnp.bfloat16), "rep", 2, reps)
    from_x = swap(pick(two, 1 - at_x, 1).astype(jnp.bfloat16), "rep", 1, reps)
    one = pick(one, at_y, 1) + from_y.astype(jnp.float32)
    two = pick(two, at_x, 1) + from_x.astype(jnp.float32)
    square = jnp.stack([one, two], 1)
    owned = pick(square, at_z, 0)
    for step in range(1, chips):
        going = pick(square, (at_z + step) % chips, 0).astype(jnp.bfloat16)
        owned = owned + turn(going, 2 * step, shards).astype(jnp.float32)
    owned = owned.astype(jnp.bfloat16)
    one, two = owned[0], owned[1]
    far_x = swap(one, "rep", 2, reps)
    far_y = swap(two, "rep", 1, reps)
    pair_x = in_order(one, far_x, at_y, 0)
    pair_y = in_order(two, far_y, at_x, 0)
    other_x = swap(pair_x, "rep", 1, reps)
    other_y = swap(pair_y, "rep", 2, reps)
    whole = jnp.stack([in_order(pair_x, other_x, at_x, 0), in_order(pair_y, other_y, at_y, 0)])
    return whole.reshape(count, width)


def total_small(flat):
    shards, reps = lax.axis_size("shard"), lax.axis_size("rep")
    if not staged() or shards & (shards - 1):
        return lax.psum(flat, ("rep", "shard"))
    for axis, size in (("shard", shards), ("rep", reps)):
        bit = 1
        while bit < size:
            flat = flat + swap(flat, axis, bit, size)
            bit = 2 * bit
    return flat


def on_device(
    tokens,
    cotangent,
    lengths,
    in_weight,
    out_weight,
    small_params,
    in_first,
    in_second,
    out_first,
    out_second,
    small_first,
    small_second,
):
    segment = segment_ids(lengths[0], tokens.shape[0])
    small_rows = lax.optimization_barrier(small_params.astype(jnp.bfloat16)).astype(jnp.float32)
    stream = tokens.astype(jnp.float32)
    shards_rows = []
    for layer_idx in range(LAYERS):
        shards_rows.append(in_weight[layer_idx].astype(jnp.bfloat16))
        shards_rows.append(out_weight[layer_idx].astype(jnp.bfloat16))
    matrices = gather_all(shards_rows)
    kept_weights = [matrices[2 * n : 2 * n + 2] for n in range(LAYERS)]
    inputs_kept = []
    acts_kept = []
    for layer_idx in range(LAYERS):
        gathered = kept_weights[layer_idx]
        inputs_kept.append(stream)
        stream, kept_acts = forward_layer(
            stream, gathered[0], gathered[1], split_small(small_rows[layer_idx]), segment
        )
        acts_kept.append(kept_acts)
    result = stream.astype(jnp.bfloat16)
    upstream = cotangent * (segment < SEQ_DEV).astype(jnp.float32)[:, None]
    in_rows = [None] * LAYERS
    out_rows = [None] * LAYERS
    small_sums = [None] * LAYERS
    for layer_idx in reversed(range(LAYERS)):
        in_wide, out_wide = kept_weights[layer_idx]
        normed, projected, mixed_out = acts_kept[layer_idx]
        small_pieces = split_small(small_rows[layer_idx])
        grad_bf = upstream.astype(jnp.bfloat16)
        grad_mixed = lax.dot_general(
            grad_bf, out_wide, (((1,), (1,)), ((), ())), preferred_element_type=jnp.float32
        )

        def local_mixer(proj_in, *small_in):
            return ssd_mixer(proj_in, *small_in, segment)

        unused, pull_back = jax.vjp(local_mixer, projected, *small_pieces[1:])
        pulled = pull_back(grad_mixed)
        grad_proj = pulled[0].astype(jnp.bfloat16)
        grad_normed = lax.dot_general(
            grad_proj, in_wide, (((1,), (1,)), ((), ())), preferred_element_type=jnp.float32
        )
        unused_norm, pull_norm = jax.vjp(prenorm, inputs_kept[layer_idx], small_pieces[0])
        grad_stream, grad_gain = pull_norm(grad_normed)
        small_flat = jnp.concatenate([grad_gain] + [term.reshape(-1) for term in pulled[1:]])

        in_rows[layer_idx] = total_rows(normed, grad_proj)
        out_rows[layer_idx] = total_rows(mixed_out, grad_bf)
        small_sums[layer_idx] = total_small(small_flat)
        upstream = upstream + grad_stream
    in_grad = jnp.stack(in_rows).astype(jnp.float32)
    out_grad = jnp.stack(out_rows).astype(jnp.float32)
    small_grad = jnp.stack(small_sums)
    new_in, new_in_first, new_in_second = adamw_update(in_weight, in_grad, in_first, in_second)
    new_out, new_out_first, new_out_second = adamw_update(
        out_weight, out_grad, out_first, out_second
    )
    new_small, new_small_first, new_small_second = adamw_update(
        small_params, small_grad, small_first, small_second
    )
    return (
        result,
        upstream,
        in_grad,
        out_grad,
        small_grad,
        new_in,
        new_out,
        new_small,
        new_in_first,
        new_in_second,
        new_out_first,
        new_out_second,
        new_small_first,
        new_small_second,
    )


def solution(mesh):
    return jax.shard_map(
        on_device,
        mesh=mesh,
        in_specs=(
            P(("rep", "shard"), None),
            P(("rep", "shard"), None),
            P(("rep", "shard"), None),
            P(None, "shard", None),
            P(None, "shard", None),
            P(),
            P(None, "shard", None),
            P(None, "shard", None),
            P(None, "shard", None),
            P(None, "shard", None),
            P(),
            P(),
        ),
        out_specs=(
            P(("rep", "shard"), None),
            P(("rep", "shard"), None),
            P(None, "shard", None),
            P(None, "shard", None),
            P(),
            P(None, "shard", None),
            P(None, "shard", None),
            P(),
            P(None, "shard", None),
            P(None, "shard", None),
            P(None, "shard", None),
            P(None, "shard", None),
            P(),
            P(),
        ),
        check_vma=False,
    )
```

```python
import math

import jax
import jax.numpy as jnp
from jax import lax
from jax.experimental import pallas as pl
from jax.experimental.pallas import tpu as pltpu
from jax.sharding import PartitionSpec as P

D = 1024
HEADS = 16
HEAD_DIM = 64
INNER = 1024
STATE = 128
KERNEL = 4
LAYERS = 2
SEQ_DEV = 4
CONV_CH = 1280


norm_eps = 1e-05
beta_one = 0.9
beta_two = 0.95
adam_eps = 1e-08
learning_rate = 0.1
weight_decay = 0.1
step_count = 3


def small_shapes():
    return [(D,), (CONV_CH, KERNEL), (CONV_CH,), (HEADS,), (HEADS,), (HEADS,), (INNER,)]


def split_small(flat_row):
    pieces = []
    offset = 0
    for piece_dims in small_shapes():
        length = math.prod(piece_dims)
        pieces.append(flat_row[offset : offset + length].reshape(piece_dims))
        offset = offset + length
    return pieces


def segment_ids(seq_lens, row_count):
    seq_ends = jnp.cumsum(seq_lens)
    places = jnp.arange(row_count, dtype=jnp.int32)
    return jnp.sum((places[:, None] >= seq_ends[None, :]).astype(jnp.int32), axis=1)


def prenorm(stream, gain):
    return stream * lax.rsqrt(jnp.mean(stream * stream, axis=-1, keepdims=True) + norm_eps) * gain


def ssd_mixer(projected, conv_weight, conv_bias, dt_bias, a_log, skip, norm_gain, segment):
    row_count = projected.shape[0]
    gate_in = projected[:, :INNER]
    conv_in = projected[:, INNER : INNER + CONV_CH]
    dt_raw = projected[:, INNER + CONV_CH :]
    conv_out = conv_bias[None, :] + conv_weight[None, :, KERNEL - 1] * conv_in
    for lag_steps in range(1, KERNEL):
        shifted = jnp.concatenate(
            [jnp.zeros((lag_steps, CONV_CH), jnp.float32), conv_in[:-lag_steps]], axis=0
        )
        earlier = jnp.concatenate(
            [jnp.full((lag_steps,), -1, jnp.int32), segment[:-lag_steps]], axis=0
        )
        conv_out = conv_out + conv_weight[None, :, KERNEL - 1 - lag_steps] * jnp.where(
            (earlier == segment)[:, None], shifted, 0.0
        )
    activated = jax.nn.silu(conv_out)
    values = activated[:, :INNER].reshape(row_count, HEADS, HEAD_DIM)
    b_state = activated[:, INNER : INNER + STATE]
    c_state = activated[:, INNER + STATE :]
    step_size = jax.nn.softplus(dt_raw + dt_bias[None, :])
    log_decay = -jnp.exp(a_log)[None, :] * step_size
    cumulative = jnp.cumsum(log_decay, axis=0)
    scores = jnp.dot(c_state, b_state.T, precision=lax.Precision.HIGHEST)
    places = jnp.arange(row_count, dtype=jnp.int32)
    allowed = ((places[:, None] >= places[None, :]) & (segment[:, None] == segment[None, :]))[None]
    spread = cumulative.T[:, :, None] - cumulative.T[:, None, :]
    decays = jnp.where(allowed, jnp.exp(jnp.where(allowed, spread, 0.0)), 0.0)
    kernel_mat = decays * scores[None] * step_size.T[:, None, :]
    output = jnp.einsum("hts,shp->thp", kernel_mat, values, precision=lax.Precision.HIGHEST)
    output = output + skip[None, :, None] * values
    gated_out = output.reshape(row_count, INNER) * jax.nn.silu(gate_in)
    return (
        gated_out
        * lax.rsqrt(jnp.mean(gated_out * gated_out, axis=-1, keepdims=True) + norm_eps)
        * norm_gain
    )


def forward_layer(stream, in_wide, out_wide, small_pieces, segment):
    normed = prenorm(stream, small_pieces[0]).astype(jnp.bfloat16)
    projected = jnp.dot(normed, in_wide, preferred_element_type=jnp.float32)
    mixed_out = ssd_mixer(projected, *small_pieces[1:], segment).astype(jnp.bfloat16)
    result = stream + jnp.dot(mixed_out, out_wide, preferred_element_type=jnp.float32)
    return (result, (normed, projected, mixed_out))


def adamw_update(params, grad_rows, first_state, second_state):
    new_first = beta_one * first_state + (1.0 - beta_one) * grad_rows
    new_second = beta_two * second_state + (1.0 - beta_two) * grad_rows * grad_rows
    first_hat = new_first / (1.0 - beta_one**step_count)
    second_hat = new_second / (1.0 - beta_two**step_count)
    new_params = params - learning_rate * (
        first_hat / (jnp.sqrt(second_hat) + adam_eps) + weight_decay * params
    )
    return (new_params, new_first, new_second)


def swap(value, axis, bit, size):
    return lax.ppermute(value, axis, [(spot, spot ^ bit) for spot in range(size)])


def turn(value, step, size):
    return lax.ppermute(value, "shard", [(spot, (spot + step) % size) for spot in range(size)])


def pick(value, index, axis):
    return lax.dynamic_index_in_dim(value, index, axis, keepdims=False)


def in_order(mine, other, index, axis):
    first = jnp.where(index == 0, mine, other)
    second = jnp.where(index == 0, other, mine)
    return jnp.stack([first, second], axis)


def places():
    rep, shard = lax.axis_index("rep"), lax.axis_index("shard")
    return rep % 2, rep // 2, shard // 2, shard % 2


def staged():
    return lax.axis_size("rep") == 4 and lax.axis_size("shard") % 2 == 0


def mesh_place(at_x, at_y, at_z, at_core):
    return (at_y * 2 + at_x, at_z * 2 + at_core)


def push(source, target, send, recv, slot, place):
    copy = pltpu.make_async_remote_copy(
        src_ref=source,
        dst_ref=target,
        send_sem=send.at[slot],
        recv_sem=recv.at[slot],
        device_id=place,
        device_id_type=pl.DeviceIdType.MESH,
    )
    copy.start()
    return copy


def greet(partners):
    barrier = pltpu.get_barrier_semaphore()
    for place in partners:
        pl.semaphore_signal(
            barrier, inc=1, device_id=place, device_id_type=pl.DeviceIdType.MESH
        )
    pl.semaphore_wait(barrier, len(partners))


def neighbours(chips):
    at_x, at_y, at_z, at_core = places()
    next_x = mesh_place(1 - at_x, at_y, at_z, at_core)
    next_y = mesh_place(at_x, 1 - at_y, at_z, at_core)
    twin = mesh_place(at_x, at_y, at_z, 1 - at_core)
    along = [
        mesh_place(at_x, at_y, lax.rem(at_z + step, chips), at_core) for step in range(1, chips)
    ]
    return next_x, next_y, twin, along


def gather_kernel(chips, count, *refs):
    own, whole = refs[:count], refs[count : 2 * count]
    send, recv, local = refs[2 * count :]
    at_x, at_y, at_z, at_core = places()
    next_x, next_y, twin, along = neighbours(chips)
    greet([next_x, next_y, twin] + along)
    first, second = (at_x, at_y), (at_y, at_x)
    inner, outer = (next_y, next_x), (next_x, next_y)
    started = []
    slots = iter(range(send.shape[0]))

    def go(source, target, place):
        copy = push(source, target, send, recv, next(slots), place)
        started.append(copy)
        return copy

    kept, level_one, level_four = [], {}, []
    for k in range(count):
        for step in range(1, chips):
            level_one[k, step] = [
                go(
                    own[k].at[h, first[h], second[h]],
                    whole[k].at[at_z, at_core, h, first[h], second[h]],
                    along[step - 1],
                )
                for h in range(2)
            ]
    for k in range(count):
        keep = pltpu.make_async_copy(own[k], whole[k].at[at_z, at_core], local.at[k])
        keep.start()
        kept.append(keep)
        level_four.append(go(own[k], whole[k].at[at_z, at_core], twin))
    units = [(k, step) for k in range(count) for step in range(1, chips)]
    level_two, level_three = {}, {}
    for turn_index in range(len(units) + 2):
        if turn_index < len(units):
            k, step = unit = units[turn_index]
            origin = lax.rem(at_z + chips - step, chips)
            level_two[unit] = []
            for h in range(2):
                level_one[unit][h].wait_recv()
                piece = whole[k].at[origin, at_core, h, first[h], second[h]]
                level_two[unit].append(go(piece, piece, inner[h]))
        if 0 <= turn_index - 1 < len(units):
            k, step = unit = units[turn_index - 1]
            origin = lax.rem(at_z + chips - step, chips)
            level_three[unit] = []
            for h in range(2):
                level_two[unit][h].wait_recv()
                piece = whole[k].at[origin, at_core, h, first[h]]
                level_three[unit].append(go(piece, piece, outer[h]))
        if 0 <= turn_index - 2:
            k, step = unit = units[turn_index - 2]
            origin = lax.rem(at_z + chips - step, chips)
            for h in range(2):
                level_three[unit][h].wait_recv()
            piece = whole[k].at[origin, at_core]
            level_four.append(go(piece, piece, twin))
    for copy in level_four:
        copy.wait_recv()
    for copy in started:
        copy.wait_send()
    for keep in kept:
        keep.wait()


def gather_all(shards_rows):
    if not staged():
        return [lax.all_gather(rows, "shard", axis=0, tiled=True) for rows in shards_rows]
    shards = lax.axis_size("shard")
    chips = shards // 2
    count = len(shards_rows)
    own = [rows.reshape(2, 2, 2, rows.shape[0] // 8, rows.shape[1]) for rows in shards_rows]
    copies = count * (7 * (chips - 1) + 1)
    whole = pl.pallas_call(
        lambda *refs: gather_kernel(chips, count, *refs),
        out_shape=[jax.ShapeDtypeStruct((chips, 2) + rows.shape, rows.dtype) for rows in own],
        in_specs=[pl.BlockSpec(memory_space=pltpu.VMEM)] * count,
        out_specs=[pl.BlockSpec(memory_space=pl.ANY)] * count,
        scratch_shapes=[
            pltpu.SemaphoreType.DMA((copies,)),
            pltpu.SemaphoreType.DMA((copies,)),
            pltpu.SemaphoreType.DMA((count,)),
        ],
        compiler_params=pltpu.CompilerParams(collective_id=0, has_side_effects=True),
        name="gather_all",
    )(*own)
    return [full.reshape(-1, rows.shape[1]) for full, rows in zip(whole, shards_rows)]


def total_kernel(chips, count, *refs):
    terms, owned = refs[:count], refs[count : 2 * count]
    from_twin, from_outer, from_inner, from_along, mine = (
        refs[(2 + n) * count : (3 + n) * count] for n in range(5)
    )
    send, recv = refs[7 * count :]
    at_x, at_y, at_z, at_core = places()
    next_x, next_y, twin, along = neighbours(chips)
    across = mesh_place(1 - at_x, 1 - at_y, at_z, at_core)
    greet([next_x, next_y, across, twin] + along)
    first, second = (at_x, at_y), (at_y, at_x)
    inner, outer = (next_y, next_x), (next_x, next_y)
    started = []
    slots = iter(range(send.shape[0]))

    def go(source, target, place):
        copy = push(source, target, send, recv, next(slots), place)
        started.append(copy)
        return copy

    def add(one, two):
        return (one.astype(jnp.float32) + two.astype(jnp.float32)).astype(jnp.bfloat16)

    steps = list(range(1, chips)) + [0]
    units = [(k, step) for k in range(count) for step in steps]
    goal = {step: lax.rem(at_z + step, chips) for step in steps}
    level_zero, level_one, level_two, level_three, level_four = {}, {}, {}, {}, []
    for k, step in units:
        level_zero[k, step] = go(
            terms[k].at[goal[step], 1 - at_core], from_twin[k].at[goal[step]], twin
        )
    for turn_index in range(len(units) + 4):
        if turn_index < len(units):
            k, step = unit = units[turn_index]
            spot = goal[step]
            level_zero[unit].wait_recv()
            for h in range(2):
                for a in range(2):
                    from_twin[k][spot, h, a] = add(
                        from_twin[k][spot, h, a], terms[k][spot, at_core, h, a]
                    )
            level_one[unit] = [
                go(from_twin[k].at[spot, h, 1 - first[h]], from_outer[k].at[spot, h], outer[h])
                for h in range(2)
            ]
        if 0 <= turn_index - 1 < len(units):
            k, step = unit = units[turn_index - 1]
            spot = goal[step]
            level_two[unit] = []
            for h in range(2):
                level_one[unit][h].wait_recv()
                from_outer[k][spot, h] = add(
                    from_outer[k][spot, h], from_twin[k][spot, h, first[h]]
                )
                level_two[unit].append(
                    go(
                        from_outer[k].at[spot, h, 1 - second[h]],
                        from_inner[k].at[spot, h],
                        inner[h],
                    )
                )
        if 0 <= turn_index - 2 < len(units):
            k, step = unit = units[turn_index - 2]
            spot = goal[step]
            for h in range(2):
                level_two[unit][h].wait_recv()
                from_inner[k][spot, h] = add(
                    from_inner[k][spot, h], from_outer[k][spot, h, second[h]]
                )
            if step:
                level_three[unit] = go(
                    from_inner[k].at[spot], from_along[k].at[step - 1], along[step - 1]
                )
        if 0 <= turn_index - 4 and units[turn_index - 4][1] == 0:
            k = units[turn_index - 4][0]
            total = from_inner[k][at_z].astype(jnp.float32)
            for step in range(1, chips):
                level_three[k, step].wait_recv()
                total = total + from_along[k][step - 1].astype(jnp.float32)
            mine[k][...] = total.astype(jnp.bfloat16)
            for h in range(2):
                owned[k][h, first[h], second[h]] = mine[k][h]
                for place in (next_x, next_y, across):
                    level_four.append(
                        go(mine[k].at[h], owned[k].at[h, first[h], second[h]], place)
                    )
    for copy in level_four:
        copy.wait_recv()
    for copy in started:
        copy.wait_send()


def total_all(pairs):
    wholes = [
        lax.dot_general(left, right, (((0,), (0,)), ((), ())), preferred_element_type=jnp.float32)
        for left, right in pairs
    ]
    if not staged():
        parts = [
            lax.psum_scatter(whole, "shard", scatter_dimension=0, tiled=True) for whole in wholes
        ]
        return lax.psum(parts, "rep")
    shards = lax.axis_size("shard")
    chips = shards // 2
    count = len(pairs)
    rows = wholes[0].shape[0] // shards
    widths = [whole.shape[1] for whole in wholes]
    terms = [
        whole.astype(jnp.bfloat16).reshape(chips, 2, 2, 2, 2, rows // 8, width)
        for whole, width in zip(wholes, widths)
    ]
    copies = count * (6 * chips - 1 + 6)

    def room(*lead):
        return [pltpu.VMEM(lead + (rows // 8, width), jnp.bfloat16) for width in widths]

    owned = pl.pallas_call(
        lambda *refs: total_kernel(chips, count, *refs),
        out_shape=[jax.ShapeDtypeStruct((2, 2, 2, rows // 8, width), jnp.bfloat16) for width in widths],
        in_specs=[pl.BlockSpec(memory_space=pltpu.VMEM)] * count,
        out_specs=[pl.BlockSpec(memory_space=pltpu.VMEM)] * count,
        scratch_shapes=room(chips, 2, 2, 2)
        + room(chips, 2, 2)
        + room(chips, 2)
        + room(chips - 1, 2)
        + room(2)
        + [pltpu.SemaphoreType.DMA((copies,)), pltpu.SemaphoreType.DMA((copies,))],
        compiler_params=pltpu.CompilerParams(collective_id=1, has_side_effects=True),
        name="total_all",
    )(*terms)
    return [part.reshape(rows, width).astype(jnp.float32) for part, width in zip(owned, widths)]


def total_small(flat):
    shards, reps = lax.axis_size("shard"), lax.axis_size("rep")
    if not staged() or shards & (shards - 1):
        return lax.psum(flat, ("rep", "shard"))
    for axis, size in (("shard", shards), ("rep", reps)):
        bit = 1
        while bit < size:
            flat = flat + swap(flat, axis, bit, size)
            bit = 2 * bit
    return flat


def on_device(
    tokens,
    cotangent,
    lengths,
    in_weight,
    out_weight,
    small_params,
    in_first,
    in_second,
    out_first,
    out_second,
    small_first,
    small_second,
):
    segment = segment_ids(lengths[0], tokens.shape[0])
    small_rows = lax.optimization_barrier(small_params.astype(jnp.bfloat16)).astype(jnp.float32)
    stream = tokens.astype(jnp.float32)
    shards_rows = []
    for layer_idx in range(LAYERS):
        shards_rows.append(in_weight[layer_idx].astype(jnp.bfloat16))
        shards_rows.append(out_weight[layer_idx].astype(jnp.bfloat16))
    matrices = gather_all(shards_rows)
    kept_weights = [matrices[2 * n : 2 * n + 2] for n in range(LAYERS)]
    inputs_kept = []
    acts_kept = []
    for layer_idx in range(LAYERS):
        gathered = kept_weights[layer_idx]
        inputs_kept.append(stream)
        stream, kept_acts = forward_layer(
            stream, gathered[0], gathered[1], split_small(small_rows[layer_idx]), segment
        )
        acts_kept.append(kept_acts)
    result = stream.astype(jnp.bfloat16)
    upstream = cotangent * (segment < SEQ_DEV).astype(jnp.float32)[:, None]
    factors = [None] * LAYERS
    small_sums = [None] * LAYERS
    for layer_idx in reversed(range(LAYERS)):
        in_wide, out_wide = kept_weights[layer_idx]
        normed, projected, mixed_out = acts_kept[layer_idx]
        small_pieces = split_small(small_rows[layer_idx])
        grad_bf = upstream.astype(jnp.bfloat16)
        grad_mixed = lax.dot_general(
            grad_bf, out_wide, (((1,), (1,)), ((), ())), preferred_element_type=jnp.float32
        )

        def local_mixer(proj_in, *small_in):
            return ssd_mixer(proj_in, *small_in, segment)

        unused, pull_back = jax.vjp(local_mixer, projected, *small_pieces[1:])
        pulled = pull_back(grad_mixed)
        grad_proj = pulled[0].astype(jnp.bfloat16)
        grad_normed = lax.dot_general(
            grad_proj, in_wide, (((1,), (1,)), ((), ())), preferred_element_type=jnp.float32
        )
        unused_norm, pull_norm = jax.vjp(prenorm, inputs_kept[layer_idx], small_pieces[0])
        grad_stream, grad_gain = pull_norm(grad_normed)
        small_flat = jnp.concatenate([grad_gain] + [term.reshape(-1) for term in pulled[1:]])

        factors[layer_idx] = [(normed, grad_proj), (mixed_out, grad_bf)]
        small_sums[layer_idx] = small_flat
        upstream = upstream + grad_stream
    small_grad = total_small(jnp.stack(small_sums))
    owned = total_all([pair for n in reversed(range(LAYERS)) for pair in factors[n]])
    in_grad = jnp.stack(owned[0::2][::-1])
    out_grad = jnp.stack(owned[1::2][::-1])
    new_in, new_in_first, new_in_second = adamw_update(in_weight, in_grad, in_first, in_second)
    new_out, new_out_first, new_out_second = adamw_update(
        out_weight, out_grad, out_first, out_second
    )
    new_small, new_small_first, new_small_second = adamw_update(
        small_params, small_grad, small_first, small_second
    )
    return (
        result,
        upstream,
        in_grad,
        out_grad,
        small_grad,
        new_in,
        new_out,
        new_small,
        new_in_first,
        new_in_second,
        new_out_first,
        new_out_second,
        new_small_first,
        new_small_second,
    )


def solution(mesh):
    return jax.shard_map(
        on_device,
        mesh=mesh,
        in_specs=(
            P(("rep", "shard"), None),
            P(("rep", "shard"), None),
            P(("rep", "shard"), None),
            P(None, "shard", None),
            P(None, "shard", None),
            P(),
            P(None, "shard", None),
            P(None, "shard", None),
            P(None, "shard", None),
            P(None, "shard", None),
            P(),
            P(),
        ),
        out_specs=(
            P(("rep", "shard"), None),
            P(("rep", "shard"), None),
            P(None, "shard", None),
            P(None, "shard", None),
            P(),
            P(None, "shard", None),
            P(None, "shard", None),
            P(),
            P(None, "shard", None),
            P(None, "shard", None),
            P(None, "shard", None),
            P(None, "shard", None),
            P(),
            P(),
        ),
        check_vma=False,
    )
```
